32 devices in a mesh: band: 16 (over z, x, core), lev: 2 (over y).
Axes of the slice: x: 2, y: 2, z: 4, core: 2. Of those that a mesh axis runs over, the one named last changes fastest.
Arguments:
- air_heat_state: bfloat16 [8, 2, 512, 4096], P('lev', None, 'band'), may hold values from -6 to 6
- mixing_coefficient: bfloat16 [2, 512, 4096], P(None, 'band'), may hold values from 0.049804688 to 0.19921875
- layer_depth_factor: float32 [8], P('lev'), may hold values from 0.3 to 0.8
- weighted_polynomial_table: bfloat16 [512, 320, 641], P('band'), may hold values from -0.25 to 0.25
- wavenumber_to_mode_degree: int32 [320], replicated, may hold values from 0 to 319, each once
Outputs:
- smoothed: bfloat16 [8, 2, 512, 4096], P('lev', None, 'band')
- spectral: float32 [8, 2, 2, 320, 641], P('lev', None, None, 'band')
The draws below stay inside these ranges and needn't reach their ends.
Inputs may be any that keep to these rules, and one draw needn't show every extreme that they name: wavenumber_to_mode_degree holds every pair row 0 to 319 once; pair row p holds wavenumbers p and 639 - p.
All inputs are finite; a program needn't handle non-finite values.
Results may differ from the reference program's by a relative error of at most 0.009.
Values may be sent and summed in bfloat16 or wider, within the bound.
No kernel may reach another device: no remote copies, remote signals or barrier semaphores. Data moves between devices by JAX's collectives and lax.ppermute only.
A program may use at most 128 MiB of HBM per device.

```python
import math
import jax
import jax.numpy as jnp
from jax import lax

ZONAL_POINTS = 4096
MERIDIAN_STEPS = 1024
K = 640
VERTICAL_LAYERS = 8


def raised(values, own_key, source, target, blocks, factor):
    owner, partner = [(jnp.arange(values.shape[position]) // (values.shape[position] // blocks)).reshape([-1 if axis == position else 1 for axis in range(values.ndim)]) for position in (source, target)]
    chosen = jax.random.permutation(own_key, blocks)[partner]
    strong = (owner == chosen) | (owner == (partner + blocks // 2) % blocks)
    return jnp.where(strong, factor * values, values)


def levels(key, shape, pieces, least, high):
    factor_of = 1.0
    for position, blocks in pieces:
        steps = jax.random.uniform(jax.random.fold_in(jax.random.fold_in(key, 6), position), (blocks,), jnp.float32, least / len(pieces), high / len(pieces))
        factor_of = factor_of * jnp.repeat(jnp.exp(steps), shape[position] // blocks).reshape((-1,) + (1,) * (len(shape) - 1 - position))
    return factor_of


def noise(own_key, extent, scale, reach, cuts=(), held_as=jnp.bfloat16):
    gain = levels(own_key, extent, cuts, -0.22, 0.18) if cuts else 1.0
    values = jax.random.normal(own_key, extent, jnp.float32) * scale * gain
    return jnp.minimum(jnp.maximum(values, -reach), reach).astype(held_as)


def gaussian_with(key, dims, width, bound, cuts, heavy, kind=jnp.bfloat16):
    result = width * jax.random.normal(key, dims, jnp.float32)
    if cuts:
        result = result * levels(key, dims, cuts, -0.22, 0.18)
    return jnp.clip(raised(result, jax.random.fold_in(key, 3), *heavy), -bound, bound).astype(kind)


def setup_inputs(seed: int = 0) -> dict:
    streams_of = jax.random.split(jax.random.key(seed), 6)
    return {
        "air_heat_state": noise(streams_of[0], (VERTICAL_LAYERS, 2, MERIDIAN_STEPS // 2, ZONAL_POINTS), 1.0, 6.0, ((0, 2), (2, 16))),
        "mixing_coefficient": jnp.clip(jnp.exp(math.log(0.19921875) - 1.3862944 * jax.random.uniform(streams_of[1], (2, MERIDIAN_STEPS // 2, ZONAL_POINTS), jnp.float32) ** levels(streams_of[1], (2, MERIDIAN_STEPS // 2, ZONAL_POINTS), ((1, 16),), -0.2, 0.2)), 0.049804688, 0.19921875).astype(jnp.bfloat16),
        "layer_depth_factor": jnp.clip(jnp.exp(math.log(0.8) - 0.98082923 * jax.random.uniform(streams_of[2], (VERTICAL_LAYERS,), jnp.float32) ** levels(streams_of[2], (VERTICAL_LAYERS,), ((0, 2),), -0.2, 0.2)), 0.3, 0.8),
        "weighted_polynomial_table": gaussian_with(streams_of[3], (MERIDIAN_STEPS // 2, K // 2, K + 1), MERIDIAN_STEPS ** -0.5, 0.25, ((0, 16),), (0, 1, 16, 2.0)),
        "wavenumber_to_mode_degree": jax.random.permutation(streams_of[4], K // 2).astype(jnp.int32),
    }


def pair_terms(products, pair_index, columns):
    count_pairs = products.shape[0]
    products = products.reshape(count_pairs, 4, products.shape[1] // 4, columns)
    column_ids = jnp.arange(columns, dtype=jnp.int32)[None, :]
    pair_ids = pair_index.astype(jnp.int32)[:, None]
    first_part = column_ids < columns - 1 - pair_ids
    parity = jnp.where(first_part, column_ids % 2, (column_ids + pair_ids) % 2)
    signs = (1 - 2 * parity).astype(products.dtype)[:, None, :]
    first_part = first_part[:, None, :]
    return jnp.where(first_part, products[:, 0] + signs * products[:, 1], products[:, 2] + signs * products[:, 3])

def reference(air_heat_state, mixing_coefficient, layer_depth_factor, weighted_polynomial_table, wavenumber_to_mode_degree):
    half_rows = MERIDIAN_STEPS // 2
    physical_space_values = air_heat_state.astype(jnp.float32)
    kappa_field = mixing_coefficient.astype(jnp.float32)
    row_ids = jnp.arange(half_rows, dtype=jnp.float32)
    centre = jnp.sin((row_ids + 0.5) * (math.pi / MERIDIAN_STEPS))[:, None]
    upper_face = jnp.sin((row_ids + 1.0) * (math.pi / MERIDIAN_STEPS))[:, None]
    lower_face = jnp.sin(row_ids * (math.pi / MERIDIAN_STEPS))[:, None]
    eastward = jnp.roll(physical_space_values, -1, axis=3)
    westward = jnp.roll(physical_space_values, 1, axis=3)
    poleward = jnp.concatenate([jnp.zeros_like(physical_space_values[:, :, :1]), physical_space_values[:, :, :-1]], axis=2)
    equatorward = jnp.concatenate([physical_space_values[:, :, 1:], physical_space_values[:, ::-1, -1:]], axis=2)
    meridional = (upper_face * (equatorward - physical_space_values) - lower_face * (physical_space_values - poleward)) / centre
    smoothed = (physical_space_values + kappa_field[None] * (eastward - 2.0 * physical_space_values + westward + meridional)).astype(jnp.bfloat16)
    weighted = layer_depth_factor.astype(jnp.float32)[:, None, None, None] * smoothed.astype(jnp.float32)
    from_ground = jnp.cumsum(weighted[::-1], axis=0)[::-1]
    geopotential = (from_ground - 0.5 * weighted).astype(jnp.bfloat16)
    grid = jnp.stack([smoothed, geopotential], axis=1).astype(jnp.float32)
    spectrum = jnp.fft.rfft(grid, axis=-1)[..., :K] / math.sqrt(ZONAL_POINTS)
    fourier = jnp.stack([jnp.real(spectrum), jnp.imag(spectrum)], axis=2).astype(jnp.bfloat16)
    half_k = K // 2
    channels = VERTICAL_LAYERS * 4
    north = fourier[:, :, :, 0].reshape(channels, half_rows, K)
    south = fourier[:, :, :, 1].reshape(channels, half_rows, K)
    stacked = jnp.stack([north[..., :half_k], south[..., :half_k], north[..., ::-1][..., :half_k], south[..., ::-1][..., :half_k]], axis=0)
    arranged = jnp.transpose(stacked, (3, 0, 1, 2)).reshape(half_k, 4 * channels, half_rows).astype(jnp.float32)

    def pair_block(block_start):
        coeff_block = lax.dynamic_slice_in_dim(arranged, block_start, 32, 0)
        table_block = lax.dynamic_slice_in_dim(weighted_polynomial_table, block_start, 32, 1).astype(jnp.float32)
        products = jnp.einsum('pkj,jpq->pkq', coeff_block, table_block)
        return pair_terms(products, block_start + jnp.arange(32, dtype=jnp.int32), K + 1)
    starts = jnp.arange(0, half_k, 32, dtype=jnp.int32)
    by_pair = lax.map(pair_block, starts).reshape(half_k, channels, K + 1)
    by_slot = jnp.take(by_pair, wavenumber_to_mode_degree.astype(jnp.int32), axis=0)
    spectral = jnp.transpose(by_slot.reshape(half_k, VERTICAL_LAYERS, 2, 2, K + 1), (1, 2, 3, 0, 4))
    return (smoothed, spectral)
```

```python
import functools
import math

import jax
import jax.numpy as jnp
import numpy as np
from jax import lax
from jax.experimental import pallas as pl
from jax.experimental.pallas import tpu as pltpu
from jax.sharding import PartitionSpec as P

GROUP = 8
LANES = 128


def edge_kernel(first_ref, last_ref, head_ref, tail_ref):
    head_ref[...] = first_ref[:, :, 0, :]
    tail_ref[...] = last_ref[:, :, last_ref.shape[2] - 1, :]


def edges(air):
    levels, _, rows, lon = air.shape
    tile = min(8, rows)
    return pl.pallas_call(
        edge_kernel,
        grid=(1,),
        in_specs=[
            pl.BlockSpec((levels, 2, tile, lon), lambda i: (0, 0, 0, 0)),
            pl.BlockSpec((levels, 2, tile, lon), lambda i: (0, 0, rows // tile - 1, 0)),
        ],
        out_specs=[pl.BlockSpec((levels, 2, lon), lambda i: (0, 0, 0))] * 2,
        out_shape=[jax.ShapeDtypeStruct((levels, 2, lon), air.dtype)] * 2,
        name="edges",
    )(air, air)


def wave_kernel(base_cos, base_sin, step_cos, step_sin, out_ref):
    cos, sin = base_cos[0], base_sin[0]
    turn_cos, turn_sin = step_cos[0], step_sin[0]
    lanes = cos.shape[-1]
    for block in range(out_ref.shape[-1] // lanes):
        at = slice(block * lanes, (block + 1) * lanes)
        out_ref[0, 0, :, at] = cos.astype(out_ref.dtype)
        out_ref[0, 1, :, at] = sin.astype(out_ref.dtype)
        cos, sin = cos * turn_cos - sin * turn_sin, sin * turn_cos + cos * turn_sin


def wave_table(lon, top):
    half, count, lanes = lon // 2, top // 4, 128
    index = np.arange(count)
    base, turn = [], []
    for which in range(2):
        for parity in range(2):
            pair = 2 * index + parity
            wave = pair if which == 0 else top - 1 - pair
            phase = wave[:, None] * np.arange(lanes)[None, :] % lon
            base.append(phase * (2.0 * math.pi / lon))
            phase = np.broadcast_to(wave[:, None] * lanes % lon, phase.shape)
            turn.append(phase * (2.0 * math.pi / lon))
    base, turn = np.stack(base), np.stack(turn)
    scale = 1.0 / math.sqrt(lon)
    tables = [
        jnp.asarray(table, jnp.float32)
        for table in (np.cos(base) * scale, -np.sin(base) * scale, np.cos(turn), -np.sin(turn))
    ]
    spec = pl.BlockSpec((1, count // 2, lanes), lambda i, j: (i, j, 0))
    return pl.pallas_call(
        wave_kernel,
        grid=(4, 2),
        in_specs=[spec] * 4,
        out_specs=pl.BlockSpec((1, 2, count // 2, half), lambda i, j: (i, 0, j, 0)),
        out_shape=jax.ShapeDtypeStruct((4, 2, count, half), jnp.bfloat16),
        cost_estimate=pl.CostEstimate(
            flops=4 * 2 * count * half * 3, bytes_accessed=4 * 2 * count * half * 2, transcendentals=0
        ),
        name="waves",
    )(*tables)


def smooth_kernel(
    last_ref, air_ref, kappa_ref, above_ref, below_ref, up_ref, down_ref, out_ref, fold_ref, padded
):
    rows, lon = air_ref.shape[2:]
    half = lon // 2
    is_last = last_ref[0] == 1
    for side in range(2):
        padded[side, 8 : 8 + rows, :] = air_ref[0, side].astype(jnp.float32)
    for side in range(2):
        padded[side, 7:8, :] = above_ref[0, side : side + 1, :].astype(jnp.float32)
        mirrored = padded[1 - side, 7 + rows : 8 + rows, :]
        padded[side, 8 + rows : 9 + rows, :] = jnp.where(
            is_last, mirrored, below_ref[0, side : side + 1, :].astype(jnp.float32)
        )
    tile = min(16, rows)
    for start in range(0, rows, tile):
        at = slice(start, start + tile)
        up, down = up_ref[at, :], down_ref[at, :]
        both = []
        for side in range(2):
            u = padded[side, 8 + start : 8 + start + tile, :]
            poleward = padded[side, 7 + start : 7 + start + tile, :]
            equatorward = padded[side, 9 + start : 9 + start + tile, :]
            east = pltpu.roll(u, lon - 1, 1)
            west = pltpu.roll(u, 1, 1)
            change = east - 2.0 * u + west + (up * (equatorward - u) - down * (u - poleward))
            value = (u + kappa_ref[side, at, :].astype(jnp.float32) * change).astype(jnp.bfloat16)
            out_ref[0, side, at, :] = value
            both.append(value.astype(jnp.float32))
        for sign, mixed in enumerate((both[0] + both[1], both[0] - both[1])):
            near, far = mixed[:, :half], mixed[:, half:]
            fold_ref[0, sign, 0, at, :] = (near + far).astype(jnp.bfloat16)
            fold_ref[1, sign, 0, at, :] = (near - far).astype(jnp.bfloat16)


def smooth(air, kappa, above, below, up, down, is_last):
    levels, _, rows, lon = air.shape
    whole = lambda i: (0, 0)
    return pl.pallas_call(
        smooth_kernel,
        grid=(levels,),
        in_specs=[
            pl.BlockSpec(memory_space=pltpu.SMEM),
            pl.BlockSpec((1, 2, rows, lon), lambda i: (i, 0, 0, 0)),
            pl.BlockSpec((2, rows, lon), lambda i: (0, 0, 0)),
            pl.BlockSpec((1, 2, lon), lambda i: (i, 0, 0)),
            pl.BlockSpec((1, 2, lon), lambda i: (i, 0, 0)),
            pl.BlockSpec((rows, 1), whole),
            pl.BlockSpec((rows, 1), whole),
        ],
        out_specs=[
            pl.BlockSpec((1, 2, rows, lon), lambda i: (i, 0, 0, 0)),
            pl.BlockSpec((2, 2, 1, rows, lon // 2), lambda i: (0, 0, i, 0, 0)),
        ],
        out_shape=[
            jax.ShapeDtypeStruct(air.shape, jnp.bfloat16),
            jax.ShapeDtypeStruct((2, 2, levels, rows, lon // 2), jnp.bfloat16),
        ],
        scratch_shapes=[pltpu.VMEM((2, rows + 16, lon), jnp.float32)],
        cost_estimate=pl.CostEstimate(
            flops=20 * air.size, bytes_accessed=7 * air.size, transcendentals=0
        ),
        name="smooth",
    )(is_last, air, kappa, above, below, up, down)


def fourier_kernel(rows, wave_ref, fold_ref, out_ref, lines):
    which = pl.program_id(0)
    count = wave_ref.shape[2]
    width = fold_ref.shape[1]
    tiles = lines.shape[0]
    for parity in range(2):
        field = fold_ref[(which + parity) % 2]
        if width < LANES:
            spare = jnp.zeros((LANES - width, field.shape[1]), field.dtype)
            field = jnp.concatenate([field, spare], axis=0)
        waves = wave_ref[parity].reshape(2 * count, wave_ref.shape[3])
        found = lax.dot_general(
            waves, field, (((1,), (1,)), ((), ())), preferred_element_type=jnp.float32
        )
        for part in range(2):
            for tile in range(tiles):
                lines[tile, part, pl.ds(parity, count, stride=2), :] = found[
                    part * count : (part + 1) * count, tile * LANES : (tile + 1) * LANES
                ]
    values = [
        jnp.concatenate([lines[tile, part] for tile in range(tiles)], axis=1).astype(jnp.bfloat16)
        for part in range(2)
    ]
    wide = GROUP * rows
    source = lax.broadcasted_iota(jnp.int32, (tiles * LANES, wide), 0)
    target = lax.broadcasted_iota(jnp.int32, (tiles * LANES, wide), 1)
    own = lax.broadcasted_iota(jnp.int32, (1, GROUP, wide), 1) == (
        lax.broadcasted_iota(jnp.int32, (1, GROUP, wide), 2) & (GROUP - 1)
    )
    for block in range(width // rows):
        spread = jnp.where(source == block * rows + (target >> 3), 1.0, 0.0).astype(jnp.bfloat16)
        sides = []
        for part in range(2):
            copied = jnp.dot(values[part], spread, preferred_element_type=jnp.float32)
            sides.append(jnp.where(own, copied.reshape(-1, GROUP, wide), 0.0))
        out_ref[:, 0, block * 2 * GROUP : (block + 1) * 2 * GROUP, :] = jnp.concatenate(
            sides, axis=1
        ).astype(jnp.bfloat16)


def fourier_blocks(waves, folds, rows):
    _, _, count, half = waves.shape
    width = folds.shape[1]
    pairs = 2 * count
    blocks = width // rows
    wide = GROUP * rows
    return pl.pallas_call(
        functools.partial(fourier_kernel, rows),
        grid=(2,),
        in_specs=[
            pl.BlockSpec((2, 2, count, half), lambda i: (i, 0, 0, 0)),
            pl.BlockSpec((2, width, half), lambda i: (0, 0, 0)),
        ],
        out_specs=pl.BlockSpec((pairs // GROUP, 1, blocks * 2 * GROUP, wide), lambda i: (0, i, 0, 0)),
        out_shape=jax.ShapeDtypeStruct((pairs // GROUP, 2, blocks * 2 * GROUP, wide), jnp.bfloat16),
        scratch_shapes=[pltpu.VMEM((pl.cdiv(width, LANES), 2, pairs, LANES), jnp.float32)],
        compiler_params=pltpu.CompilerParams(vmem_limit_bytes=60 << 20),
        cost_estimate=pl.CostEstimate(
            flops=2 * 8 * count * half * width,
            bytes_accessed=2 * (waves.size + folds.size),
            transcendentals=0,
        ),
        name="fourier",
    )(waves, folds)


def legendre_kernel(place_ref, block_ref, table_ref, out_ref, turned):
    step = pl.program_id(0)
    rows, pairs, columns = table_ref.shape
    groups = pairs // GROUP
    channels = out_ref.shape[1]
    for group in range(groups):
        table = table_ref[:, group * GROUP : (group + 1) * GROUP, :].reshape(rows * GROUP, columns)
        left = block_ref[group].reshape(4 * channels * GROUP, rows * GROUP)
        sums = jnp.dot(left, table, preferred_element_type=jnp.float32)
        sums = sums.reshape(2, 2, channels, GROUP, columns)
        first_pair = (step * groups + group) * GROUP
        pair = first_pair + lax.broadcasted_iota(jnp.int32, (GROUP, columns), 0)
        column = lax.broadcasted_iota(jnp.int32, (GROUP, columns), 1)
        first = column < columns - 1 - pair
        odd = jnp.where(first, column, column - (columns - 1) + pair) & 1
        even = (odd == 0)[None]
        chosen = jnp.where(
            first[None],
            jnp.where(even, sums[0, 0], sums[0, 1]),
            jnp.where(even, sums[1, 0], sums[1, 1]),
        )
        chosen = chosen.reshape(channels * GROUP, columns)
        for tile in range(turned.shape[0]):
            start, end = tile * LANES, min(columns, (tile + 1) * LANES)
            turned[tile, :, : end - start] = chosen[:, start:end]
        for member in range(GROUP):
            place = place_ref[first_pair + member]
            for tile in range(turned.shape[0]):
                start, end = tile * LANES, min(columns, (tile + 1) * LANES)
                value = turned[tile, pl.ds(member, channels, stride=GROUP), :]
                out_ref[place, :, start:end] = value[:, : end - start].astype(out_ref.dtype)


def legendre(places, blocks, table):
    rows, half_k, columns = table.shape
    channels = blocks.shape[1] * blocks.shape[2] // (4 * GROUP)
    pairs = 2 * GROUP
    groups = pairs // GROUP
    return pl.pallas_call(
        legendre_kernel,
        grid_spec=pltpu.PrefetchScalarGridSpec(
            num_scalar_prefetch=1,
            grid=(half_k // pairs,),
            in_specs=[
                pl.BlockSpec((groups, *blocks.shape[1:]), lambda i, s: (i, 0, 0, 0)),
                pl.BlockSpec((rows, pairs, columns), lambda i, s: (0, i, 0)),
            ],
            out_specs=pl.BlockSpec((half_k, channels, columns), lambda i, s: (0, 0, 0)),
            scratch_shapes=[pltpu.VMEM((pl.cdiv(columns, LANES), channels * GROUP, LANES), jnp.float32)],
        ),
        out_shape=jax.ShapeDtypeStruct((half_k, channels, columns), jnp.bfloat16),
        compiler_params=pltpu.CompilerParams(vmem_limit_bytes=60 << 20),
        cost_estimate=pl.CostEstimate(
            flops=2 * blocks.size * columns,
            bytes_accessed=2 * (blocks.size + table.size),
            transcendentals=0,
        ),
        name="legendre",
    )(places, blocks, table)


def reversed_bits(value, bits):
    result = jnp.zeros_like(value)
    for bit in range(bits):
        result = result * 2 + ((value >> bit) & 1)
    return result


def on_device(air, kappa, depth, table, mode_degree):
    levels, _, rows, lon = air.shape
    half_k, columns = table.shape[1:]
    band = lax.axis_index("band")
    bands = lax.axis_size("band")
    bits = bands.bit_length() - 1
    slots = half_k // bands
    steps = 2 * rows * bands

    head, tail = edges(air)
    below = lax.ppermute(head, "band", [(i + 1, i) for i in range(bands - 1)])
    above = lax.ppermute(tail, "band", [(i, i + 1) for i in range(bands - 1)])

    waves = wave_table(lon, columns - 1)
    row = (band * rows + jnp.arange(rows, dtype=jnp.int32)).astype(jnp.float32)[:, None]
    centre = jnp.sin((row + 0.5) * (math.pi / steps))
    up = jnp.sin((row + 1.0) * (math.pi / steps)) / centre
    down = jnp.sin(row * (math.pi / steps)) / centre
    is_last = (band == bands - 1).astype(jnp.int32)[None]
    slot = jnp.arange(half_k, dtype=jnp.int32)
    place = reversed_bits((slot // slots) ^ band, bits) * slots + slot % slots
    places = jnp.sum(
        jnp.where(mode_degree[None, :] == slot[:, None], place[None, :], 0), axis=1, dtype=jnp.int32
    )

    smoothed, folds = smooth(air, kappa, above, below, up, down, is_last)
    blocks = fourier_blocks(waves, folds.reshape(2, 2 * levels * rows, lon // 2), rows)
    held = [legendre(places, blocks, table)]
    count = half_k
    for bit in range(bits):
        count //= 2
        outgoing = sum(part[count : 2 * count].astype(jnp.float32) for part in held)
        held.append(
            lax.ppermute(
                outgoing.astype(jnp.bfloat16), "band", [(i, i ^ (1 << bit)) for i in range(bands)]
            )
        )
    mine = sum(part[:slots].astype(jnp.float32) for part in held)
    mine = mine.reshape(slots, levels, 2, columns)
    weighted = depth[None, :, None, None] * mine
    levs = lax.axis_size("lev")
    total = jnp.sum(weighted, axis=1)
    lower = jnp.zeros_like(total)
    if levs > 1:
        lower = lax.ppermute(total, "lev", [(i + 1, i) for i in range(levs - 1)])
        reach = 1
        while reach < levs - 1:
            lower = lower + lax.ppermute(lower, "lev", [(i + reach, i) for i in range(levs - reach)])
            reach *= 2
    potential = []
    for level in reversed(range(levels)):
        potential.append(lower + 0.5 * weighted[:, level])
        lower = lower + weighted[:, level]
    fields = jnp.stack([mine, jnp.stack(potential[::-1], axis=1)], axis=2)
    return smoothed, jnp.transpose(fields, (1, 2, 3, 0, 4))


def solution(mesh):
    placed = (
        P("lev", None, "band", None),
        P(None, "band", None),
        P("lev"),
        P("band", None, None),
        P(),
    )
    return jax.shard_map(
        on_device,
        mesh=mesh,
        in_specs=placed,
        out_specs=(P("lev", None, "band", None), P("lev", None, None, "band", None)),
        check_vma=False,
    )
```

```python
import functools
import math

import jax
import jax.numpy as jnp
import numpy as np
from jax import lax
from jax.experimental import pallas as pl
from jax.experimental.pallas import tpu as pltpu
from jax.sharding import PartitionSpec as P

GROUP = 8
LANES = 128
WIDTH = 256


def edge_kernel(first_ref, last_ref, head_ref, tail_ref):
    head_ref[...] = first_ref[:, :, 0, :]
    tail_ref[...] = last_ref[:, :, last_ref.shape[2] - 1, :]


def edges(air):
    levels, _, rows, lon = air.shape
    tile = min(8, rows)
    return pl.pallas_call(
        edge_kernel,
        grid=(1,),
        in_specs=[
            pl.BlockSpec((levels, 2, tile, lon), lambda i: (0, 0, 0, 0)),
            pl.BlockSpec((levels, 2, tile, lon), lambda i: (0, 0, rows // tile - 1, 0)),
        ],
        out_specs=[pl.BlockSpec((levels, 2, lon), lambda i: (0, 0, 0))] * 2,
        out_shape=[jax.ShapeDtypeStruct((levels, 2, lon), air.dtype)] * 2,
        compiler_params=pltpu.CompilerParams(vmem_limit_bytes=8 << 20),
        name="edges",
    )(air, air)


def wave_kernel(base_cos, base_sin, step_cos, step_sin, out_ref):
    cos, sin = base_cos[0], base_sin[0]
    turn_cos, turn_sin = step_cos[0], step_sin[0]
    lanes = cos.shape[-1]
    for block in range(out_ref.shape[-1] // lanes):
        at = slice(block * lanes, (block + 1) * lanes)
        out_ref[0, 0, :, at] = cos.astype(out_ref.dtype)
        out_ref[0, 1, :, at] = sin.astype(out_ref.dtype)
        cos, sin = cos * turn_cos - sin * turn_sin, sin * turn_cos + cos * turn_sin


def wave_table(lon, top):
    half, count, lanes = lon // 2, top // 4, 128
    index = np.arange(count)
    base, turn = [], []
    for which in range(2):
        for parity in range(2):
            pair = 2 * index + parity
            wave = pair if which == 0 else top - 1 - pair
            phase = wave[:, None] * np.arange(lanes)[None, :] % lon
            base.append(phase * (2.0 * math.pi / lon))
            phase = np.broadcast_to(wave[:, None] * lanes % lon, phase.shape)
            turn.append(phase * (2.0 * math.pi / lon))
    base, turn = np.stack(base), np.stack(turn)
    scale = 1.0 / math.sqrt(lon)
    tables = [
        jnp.asarray(table, jnp.float32)
        for table in (np.cos(base) * scale, -np.sin(base) * scale, np.cos(turn), -np.sin(turn))
    ]
    spec = pl.BlockSpec((1, count // 2, lanes), lambda i, j: (i, j, 0))
    return pl.pallas_call(
        wave_kernel,
        grid=(4, 2),
        in_specs=[spec] * 4,
        out_specs=pl.BlockSpec((1, 2, count // 2, half), lambda i, j: (i, 0, j, 0)),
        out_shape=jax.ShapeDtypeStruct((4, 2, count, half), jnp.bfloat16),
        compiler_params=pltpu.CompilerParams(vmem_limit_bytes=8 << 20),
        cost_estimate=pl.CostEstimate(
            flops=4 * 2 * count * half * 3, bytes_accessed=4 * 2 * count * half * 2, transcendentals=0
        ),
        name="waves",
    )(*tables)


def smooth_kernel(
    last_ref, air_ref, kappa_ref, above_ref, below_ref, up_ref, down_ref, out_ref, fold_ref, padded
):
    rows, lon = air_ref.shape[2:]
    half = lon // 2
    is_last = last_ref[0] == 1
    for side in range(2):
        padded[side, 8 : 8 + rows, :] = air_ref[0, side].astype(jnp.float32)
    for side in range(2):
        padded[side, 7:8, :] = above_ref[0, side : side + 1, :].astype(jnp.float32)
        mirrored = padded[1 - side, 7 + rows : 8 + rows, :]
        padded[side, 8 + rows : 9 + rows, :] = jnp.where(
            is_last, mirrored, below_ref[0, side : side + 1, :].astype(jnp.float32)
        )
    tile = min(16, rows)
    for start in range(0, rows, tile):
        at = slice(start, start + tile)
        up, down = up_ref[at, :], down_ref[at, :]
        both = []
        for side in range(2):
            u = padded[side, 8 + start : 8 + start + tile, :]
            poleward = padded[side, 7 + start : 7 + start + tile, :]
            equatorward = padded[side, 9 + start : 9 + start + tile, :]
            east = pltpu.roll(u, lon - 1, 1)
            west = pltpu.roll(u, 1, 1)
            change = east - 2.0 * u + west + (up * (equatorward - u) - down * (u - poleward))
            value = (u + kappa_ref[side, at, :].astype(jnp.float32) * change).astype(jnp.bfloat16)
            out_ref[0, side, at, :] = value
            both.append(value.astype(jnp.float32))
        for sign, mixed in enumerate((both[0] + both[1], both[0] - both[1])):
            near, far = mixed[:, :half], mixed[:, half:]
            fold_ref[0, sign, 0, at, :] = (near + far).astype(jnp.bfloat16)
            fold_ref[1, sign, 0, at, :] = (near - far).astype(jnp.bfloat16)


def smooth(air, kappa, above, below, up, down, is_last):
    levels, _, rows, lon = air.shape
    whole = lambda i: (0, 0)
    return pl.pallas_call(
        smooth_kernel,
        grid=(levels,),
        in_specs=[
            pl.BlockSpec(memory_space=pltpu.SMEM),
            pl.BlockSpec((1, 2, rows, lon), lambda i: (i, 0, 0, 0)),
            pl.BlockSpec((2, rows, lon), lambda i: (0, 0, 0)),
            pl.BlockSpec((1, 2, lon), lambda i: (i, 0, 0)),
            pl.BlockSpec((1, 2, lon), lambda i: (i, 0, 0)),
            pl.BlockSpec((rows, 1), whole),
            pl.BlockSpec((rows, 1), whole),
        ],
        out_specs=[
            pl.BlockSpec((1, 2, rows, lon), lambda i: (i, 0, 0, 0)),
            pl.BlockSpec((2, 2, 1, rows, lon // 2), lambda i: (0, 0, i, 0, 0)),
        ],
        out_shape=[
            jax.ShapeDtypeStruct(air.shape, jnp.bfloat16),
            jax.ShapeDtypeStruct((2, 2, levels, rows, lon // 2), jnp.bfloat16),
        ],
        scratch_shapes=[pltpu.VMEM((2, rows + 16, lon), jnp.float32)],
        compiler_params=pltpu.CompilerParams(vmem_limit_bytes=12 << 20),
        cost_estimate=pl.CostEstimate(
            flops=20 * air.size, bytes_accessed=7 * air.size, transcendentals=0
        ),
        name="smooth",
    )(is_last, air, kappa, above, below, up, down)


def fourier_kernel(rows, wave_ref, fold_ref, out_ref, lines):
    which = pl.program_id(0)
    count = wave_ref.shape[2]
    width = fold_ref.shape[1]
    tiles = lines.shape[0]
    for parity in range(2):
        field = fold_ref[(which + parity) % 2]
        if width < LANES:
            spare = jnp.zeros((LANES - width, field.shape[1]), field.dtype)
            field = jnp.concatenate([field, spare], axis=0)
        waves = wave_ref[parity].reshape(2 * count, wave_ref.shape[3])
        found = lax.dot_general(
            waves, field, (((1,), (1,)), ((), ())), preferred_element_type=jnp.float32
        )
        for part in range(2):
            for tile in range(tiles):
                lines[tile, part, pl.ds(parity, count, stride=2), :] = found[
                    part * count : (part + 1) * count, tile * LANES : (tile + 1) * LANES
                ]
    values = [
        jnp.concatenate([lines[tile, part] for tile in range(tiles)], axis=1).astype(jnp.bfloat16)
        for part in range(2)
    ]
    wide = GROUP * rows
    source = lax.broadcasted_iota(jnp.int32, (tiles * LANES, wide), 0)
    target = lax.broadcasted_iota(jnp.int32, (tiles * LANES, wide), 1)
    own = lax.broadcasted_iota(jnp.int32, (1, GROUP, wide), 1) == (
        lax.broadcasted_iota(jnp.int32, (1, GROUP, wide), 2) & (GROUP - 1)
    )
    for block in range(width // rows):
        spread = jnp.where(source == block * rows + (target >> 3), 1.0, 0.0).astype(jnp.bfloat16)
        sides = []
        for part in range(2):
            copied = jnp.dot(values[part], spread, preferred_element_type=jnp.float32)
            sides.append(jnp.where(own, copied.reshape(-1, GROUP, wide), 0.0))
        out_ref[:, 0, block * 2 * GROUP : (block + 1) * 2 * GROUP, :] = jnp.concatenate(
            sides, axis=1
        ).astype(jnp.bfloat16)


def fourier_blocks(waves, folds, rows):
    _, _, count, half = waves.shape
    width = folds.shape[1]
    pairs = 2 * count
    blocks = width // rows
    wide = GROUP * rows
    return pl.pallas_call(
        functools.partial(fourier_kernel, rows),
        grid=(2,),
        in_specs=[
            pl.BlockSpec((2, 2, count, half), lambda i: (i, 0, 0, 0)),
            pl.BlockSpec((2, width, half), lambda i: (0, 0, 0)),
        ],
        out_specs=pl.BlockSpec((pairs // GROUP, 1, blocks * 2 * GROUP, wide), lambda i: (0, i, 0, 0)),
        out_shape=jax.ShapeDtypeStruct((pairs // GROUP, 2, blocks * 2 * GROUP, wide), jnp.bfloat16),
        scratch_shapes=[pltpu.VMEM((pl.cdiv(width, LANES), 2, pairs, LANES), jnp.float32)],
        compiler_params=pltpu.CompilerParams(vmem_limit_bytes=24 << 20),
        cost_estimate=pl.CostEstimate(
            flops=2 * 8 * count * half * width,
            bytes_accessed=2 * (waves.size + folds.size),
            transcendentals=0,
        ),
        name="fourier",
    )(waves, folds)


def legendre_kernel(
    half_k, start, extra, place_ref, block_ref, table_ref, keep_ref, send_ref, spectra, turned, sems
):
    step = pl.program_id(0)
    rows, pairs, width = table_ref.shape
    groups = pairs // GROUP
    _, channels, kept = spectra.shape
    slots = place_ref[half_k]
    lane = lax.broadcasted_iota(jnp.int32, (channels, LANES), 1)
    for group in range(groups):
        table = table_ref[:, group * GROUP : (group + 1) * GROUP, :].reshape(rows * GROUP, width)
        left = block_ref[group].reshape(4 * channels * GROUP, rows * GROUP)
        sums = jnp.dot(left, table, preferred_element_type=jnp.float32)
        sums = sums.reshape(2, 2, channels, GROUP, width)
        first_pair = (step * groups + group) * GROUP
        pair = first_pair + lax.broadcasted_iota(jnp.int32, (GROUP, width), 0)
        column = start + lax.broadcasted_iota(jnp.int32, (GROUP, width), 1)
        first = column < 2 * half_k - pair
        odd = jnp.where(first, column, column - 2 * half_k + pair) & 1
        even = (odd == 0)[None]
        chosen = jnp.where(
            first[None],
            jnp.where(even, sums[0, 0], sums[0, 1]),
            jnp.where(even, sums[1, 0], sums[1, 1]),
        )
        chosen = chosen.reshape(channels * GROUP, width)
        for tile in range(width // LANES):
            turned[group, tile] = chosen[:, tile * LANES : (tile + 1) * LANES]
        for member in range(GROUP):
            place = place_ref[first_pair + member]
            for tile in range(kept // LANES):
                value = turned[group, tile, pl.ds(member, channels, stride=GROUP), :]
                spectra[place, :, tile * LANES : (tile + 1) * LANES] = value.astype(spectra.dtype)
            if extra:
                chunk = place // (slots + 1)
                within = place - chunk * (slots + 1)
                spare = chunk * (slots + 1) + slots
                value = turned[group, kept // LANES, pl.ds(member, channels, stride=GROUP), :]
                value = jnp.broadcast_to(value[:, :1], (channels, LANES)).astype(spectra.dtype)
                before = spectra[spare, :, :LANES]
                spectra[spare, :, :LANES] = jnp.where(lane == within, value, before)

    @pl.when(step == pl.num_programs(0) - 1)
    def _():
        count = spectra.shape[0] // 2
        send = pltpu.make_async_copy(spectra.at[pl.ds(count, count)], send_ref, sems.at[0])
        keep = pltpu.make_async_copy(spectra.at[pl.ds(0, count)], keep_ref, sems.at[1])
        send.start()
        keep.start()
        send.wait()
        keep.wait()


def legendre(places, blocks, table, start, kept, extra, total):
    rows, half_k, _ = table.shape
    channels = blocks.shape[1] * blocks.shape[2] // (4 * GROUP)
    pairs = 8 * GROUP
    groups = pairs // GROUP
    width = kept + (LANES if extra else 0)
    result = jax.ShapeDtypeStruct((total // 2, channels, kept), jnp.bfloat16)
    return pl.pallas_call(
        functools.partial(legendre_kernel, half_k, start, extra),
        grid_spec=pltpu.PrefetchScalarGridSpec(
            num_scalar_prefetch=1,
            grid=(half_k // pairs,),
            in_specs=[
                pl.BlockSpec((groups, *blocks.shape[1:]), lambda i, s: (i, 0, 0, 0)),
                pl.BlockSpec((rows, pairs, width), lambda i, s: (0, i, start // width)),
            ],
            out_specs=[pl.BlockSpec(memory_space=pl.ANY)] * 2,
            scratch_shapes=[
                pltpu.VMEM((total, channels, kept), jnp.bfloat16),
                pltpu.VMEM((groups, width // LANES, channels * GROUP, LANES), jnp.float32),
                pltpu.SemaphoreType.DMA((2,)),
            ],
        ),
        out_shape=[result, result],
        compiler_params=pltpu.CompilerParams(vmem_limit_bytes=24 << 20),
        cost_estimate=pl.CostEstimate(
            flops=2 * blocks.size * width,
            bytes_accessed=2 * (blocks.size + rows * half_k * width),
            transcendentals=0,
        ),
        name="legendre",
    )(places, blocks, table)


def reversed_bits(value, bits):
    result = jnp.zeros_like(value)
    for bit in range(bits):
        result = result * 2 + ((value >> bit) & 1)
    return result


def on_device(air, kappa, depth, table, mode_degree):
    levels, _, rows, lon = air.shape
    half_k, columns = table.shape[1:]
    band = lax.axis_index("band")
    bands = lax.axis_size("band")
    bits = bands.bit_length() - 1
    slots = half_k // bands
    steps = 2 * rows * bands

    head, tail = edges(air)
    below = lax.ppermute(head, "band", [(i + 1, i) for i in range(bands - 1)])
    above = lax.ppermute(tail, "band", [(i, i + 1) for i in range(bands - 1)])

    waves = wave_table(lon, columns - 1)
    row = (band * rows + jnp.arange(rows, dtype=jnp.int32)).astype(jnp.float32)[:, None]
    centre = jnp.sin((row + 0.5) * (math.pi / steps))
    up = jnp.sin((row + 1.0) * (math.pi / steps)) / centre
    down = jnp.sin(row * (math.pi / steps)) / centre
    is_last = (band == bands - 1).astype(jnp.int32)[None]
    slot = jnp.arange(half_k, dtype=jnp.int32)
    here = mode_degree[None, :] == slot[:, None]
    chunk = reversed_bits((slot // slots) ^ band, bits)

    def places_with(stride):
        place = chunk * stride + slot % slots
        found = jnp.sum(jnp.where(here, place[None, :], 0), axis=1, dtype=jnp.int32)
        return jnp.concatenate([found, jnp.full((1,), slots, jnp.int32)])

    smoothed, folds = smooth(air, kappa, above, below, up, down, is_last)
    blocks = fourier_blocks(waves, folds.reshape(2, 2 * levels * rows, lon // 2), rows)
    pieces = []
    top = columns - 1
    for start in range(0, top, WIDTH):
        kept = min(WIDTH, top - start)
        extra = start + kept == top
        stride = slots + 1 if extra else slots
        keep, count = legendre(
            places_with(stride), blocks, table, start, kept, extra, stride * bands
        ), stride * bands // 2
        held, outgoing = [keep[0]], keep[1]
        for bit in range(bits):
            held.append(
                lax.ppermute(outgoing, "band", [(i, i ^ (1 << bit)) for i in range(bands)])
            )
            count //= 2
            if bit < bits - 1:
                outgoing = sum(part[count : 2 * count].astype(jnp.float32) for part in held)
                outgoing = outgoing.astype(jnp.bfloat16)
        done = sum(part[:stride].astype(jnp.float32) for part in held)
        pieces.append(done[:slots])
        if extra:
            pieces.append(jnp.swapaxes(done[slots, :, :slots], 0, 1)[:, :, None])
    mine = jnp.concatenate(pieces, axis=2)
    mine = mine.reshape(slots, levels, 2, columns)
    weighted = depth[None, :, None, None] * mine
    levs = lax.axis_size("lev")
    total = jnp.sum(weighted, axis=1)
    lower = jnp.zeros_like(total)
    if levs > 1:
        lower = lax.ppermute(total, "lev", [(i + 1, i) for i in range(levs - 1)])
        reach = 1
        while reach < levs - 1:
            lower = lower + lax.ppermute(lower, "lev", [(i + reach, i) for i in range(levs - reach)])
            reach *= 2
    potential = []
    for level in reversed(range(levels)):
        potential.append(lower + 0.5 * weighted[:, level])
        lower = lower + weighted[:, level]
    fields = jnp.stack([mine, jnp.stack(potential[::-1], axis=1)], axis=2)
    return smoothed, jnp.transpose(fields, (1, 2, 3, 0, 4))


def solution(mesh):
    placed = (
        P("lev", None, "band", None),
        P(None, "band", None),
        P("lev"),
        P("band", None, None),
        P(),
    )
    return jax.shard_map(
        on_device,
        mesh=mesh,
        in_specs=placed,
        out_specs=(P("lev", None, "band", None), P("lev", None, None, "band", None)),
        check_vma=False,
    )
```

```python
import functools
import math

import jax
import jax.numpy as jnp
import numpy as np
from jax import lax
from jax.experimental import pallas as pl
from jax.experimental.pallas import tpu as pltpu
from jax.sharding import PartitionSpec as P

GROUP = 8
LANES = 128
WIDTH = 256


def edge_kernel(first_ref, last_ref, head_ref, tail_ref):
    head_ref[...] = first_ref[:, :, 0, :]
    tail_ref[...] = last_ref[:, :, last_ref.shape[2] - 1, :]


def edges(air):
    levels, _, rows, lon = air.shape
    tile = min(8, rows)
    return pl.pallas_call(
        edge_kernel,
        grid=(1,),
        in_specs=[
            pl.BlockSpec((levels, 2, tile, lon), lambda i: (0, 0, 0, 0)),
            pl.BlockSpec((levels, 2, tile, lon), lambda i: (0, 0, rows // tile - 1, 0)),
        ],
        out_specs=[pl.BlockSpec((levels, 2, lon), lambda i: (0, 0, 0))] * 2,
        out_shape=[jax.ShapeDtypeStruct((levels, 2, lon), air.dtype)] * 2,
        compiler_params=pltpu.CompilerParams(vmem_limit_bytes=8 << 20),
        name="edges",
    )(air, air)


def wave_kernel(table_ref, out_ref):
    cos, sin, turn_cos, turn_sin = (table_ref[0, kind] for kind in range(4))
    lanes = cos.shape[-1]
    for block in range(out_ref.shape[-1] // lanes):
        at = slice(block * lanes, (block + 1) * lanes)
        out_ref[0, 0, :, at] = cos.astype(out_ref.dtype)
        out_ref[0, 1, :, at] = sin.astype(out_ref.dtype)
        cos, sin = cos * turn_cos - sin * turn_sin, sin * turn_cos + cos * turn_sin


def wave_table(lon, top):
    half, count, lanes = lon // 2, top // 4, 128
    index = np.arange(count)
    base, turn = [], []
    for which in range(2):
        for parity in range(2):
            pair = 2 * index + parity
            wave = pair if which == 0 else top - 1 - pair
            phase = wave[:, None] * np.arange(lanes)[None, :] % lon
            base.append(phase * (2.0 * math.pi / lon))
            phase = np.broadcast_to(wave[:, None] * lanes % lon, phase.shape)
            turn.append(phase * (2.0 * math.pi / lon))
    base, turn = np.stack(base), np.stack(turn)
    scale = 1.0 / math.sqrt(lon)
    tables = np.stack(
        [np.cos(base) * scale, -np.sin(base) * scale, np.cos(turn), -np.sin(turn)], axis=1
    )
    return pl.pallas_call(
        wave_kernel,
        grid=(4, 2),
        in_specs=[pl.BlockSpec((1, 4, count // 2, lanes), lambda i, j: (i, 0, j, 0))],
        out_specs=pl.BlockSpec((1, 2, count // 2, half), lambda i, j: (i, 0, j, 0)),
        out_shape=jax.ShapeDtypeStruct((4, 2, count, half), jnp.bfloat16),
        compiler_params=pltpu.CompilerParams(vmem_limit_bytes=8 << 20),
        cost_estimate=pl.CostEstimate(
            flops=4 * 2 * count * half * 3, bytes_accessed=4 * 2 * count * half * 2, transcendentals=0
        ),
        name="waves",
    )(jnp.asarray(tables, jnp.float32))


def smooth_kernel(
    last_ref, air_ref, kappa_ref, above_ref, below_ref, up_ref, down_ref, out_ref, fold_ref, padded
):
    rows, lon = air_ref.shape[2:]
    half = lon // 2
    is_last = last_ref[0] == 1
    for side in range(2):
        padded[side, 8 : 8 + rows, :] = air_ref[0, side].astype(jnp.float32)
    for side in range(2):
        padded[side, 7:8, :] = above_ref[0, side : side + 1, :].astype(jnp.float32)
        mirrored = padded[1 - side, 7 + rows : 8 + rows, :]
        padded[side, 8 + rows : 9 + rows, :] = jnp.where(
            is_last, mirrored, below_ref[0, side : side + 1, :].astype(jnp.float32)
        )
    tile = min(16, rows)
    for start in range(0, rows, tile):
        at = slice(start, start + tile)
        up, down = up_ref[at, :], down_ref[at, :]
        both = []
        for side in range(2):
            u = padded[side, 8 + start : 8 + start + tile, :]
            poleward = padded[side, 7 + start : 7 + start + tile, :]
            equatorward = padded[side, 9 + start : 9 + start + tile, :]
            east = pltpu.roll(u, lon - 1, 1)
            west = pltpu.roll(u, 1, 1)
            change = east - 2.0 * u + west + (up * (equatorward - u) - down * (u - poleward))
            value = (u + kappa_ref[side, at, :].astype(jnp.float32) * change).astype(jnp.bfloat16)
            out_ref[0, side, at, :] = value
            both.append(value.astype(jnp.float32))
        for sign, mixed in enumerate((both[0] + both[1], both[0] - both[1])):
            near, far = mixed[:, :half], mixed[:, half:]
            fold_ref[0, sign, 0, at, :] = (near + far).astype(jnp.bfloat16)
            fold_ref[1, sign, 0, at, :] = (near - far).astype(jnp.bfloat16)


def smooth(air, kappa, above, below, up, down, is_last):
    levels, _, rows, lon = air.shape
    whole = lambda i: (0, 0)
    return pl.pallas_call(
        smooth_kernel,
        grid=(levels,),
        in_specs=[
            pl.BlockSpec(memory_space=pltpu.SMEM),
            pl.BlockSpec((1, 2, rows, lon), lambda i: (i, 0, 0, 0)),
            pl.BlockSpec((2, rows, lon), lambda i: (0, 0, 0)),
            pl.BlockSpec((1, 2, lon), lambda i: (i, 0, 0)),
            pl.BlockSpec((1, 2, lon), lambda i: (i, 0, 0)),
            pl.BlockSpec((rows, 1), whole),
            pl.BlockSpec((rows, 1), whole),
        ],
        out_specs=[
            pl.BlockSpec((1, 2, rows, lon), lambda i: (i, 0, 0, 0)),
            pl.BlockSpec((2, 2, 1, rows, lon // 2), lambda i: (0, 0, i, 0, 0)),
        ],
        out_shape=[
            jax.ShapeDtypeStruct(air.shape, jnp.bfloat16),
            jax.ShapeDtypeStruct((2, 2, levels, rows, lon // 2), jnp.bfloat16),
        ],
        scratch_shapes=[pltpu.VMEM((2, rows + 16, lon), jnp.float32)],
        compiler_params=pltpu.CompilerParams(vmem_limit_bytes=12 << 20),
        cost_estimate=pl.CostEstimate(
            flops=20 * air.size, bytes_accessed=7 * air.size, transcendentals=0
        ),
        name="smooth",
    )(is_last, air, kappa, above, below, up, down)


def fourier_kernel(rows, wave_ref, fold_ref, out_ref, lines):
    which = pl.program_id(0)
    count = wave_ref.shape[2]
    width = fold_ref.shape[1]
    tiles = lines.shape[0]
    for parity in range(2):
        field = fold_ref[(which + parity) % 2]
        if width < LANES:
            spare = jnp.zeros((LANES - width, field.shape[1]), field.dtype)
            field = jnp.concatenate([field, spare], axis=0)
        waves = wave_ref[parity].reshape(2 * count, wave_ref.shape[3])
        found = lax.dot_general(
            waves, field, (((1,), (1,)), ((), ())), preferred_element_type=jnp.float32
        )
        for part in range(2):
            for tile in range(tiles):
                lines[tile, part, pl.ds(parity, count, stride=2), :] = found[
                    part * count : (part + 1) * count, tile * LANES : (tile + 1) * LANES
                ]
    values = [
        jnp.concatenate([lines[tile, part] for tile in range(tiles)], axis=1).astype(jnp.bfloat16)
        for part in range(2)
    ]
    wide = GROUP * rows
    source = lax.broadcasted_iota(jnp.int32, (tiles * LANES, wide), 0)
    target = lax.broadcasted_iota(jnp.int32, (tiles * LANES, wide), 1)
    own = lax.broadcasted_iota(jnp.int32, (1, GROUP, wide), 1) == (
        lax.broadcasted_iota(jnp.int32, (1, GROUP, wide), 2) & (GROUP - 1)
    )
    for block in range(width // rows):
        spread = jnp.where(source == block * rows + (target >> 3), 1.0, 0.0).astype(jnp.bfloat16)
        sides = []
        for part in range(2):
            copied = jnp.dot(values[part], spread, preferred_element_type=jnp.float32)
            sides.append(jnp.where(own, copied.reshape(-1, GROUP, wide), 0.0))
        out_ref[:, 0, block * 2 * GROUP : (block + 1) * 2 * GROUP, :] = jnp.concatenate(
            sides, axis=1
        ).astype(jnp.bfloat16)


def fourier_blocks(waves, folds, rows):
    _, _, count, half = waves.shape
    width = folds.shape[1]
    pairs = 2 * count
    blocks = width // rows
    wide = GROUP * rows
    return pl.pallas_call(
        functools.partial(fourier_kernel, rows),
        grid=(2,),
        in_specs=[
            pl.BlockSpec((2, 2, count, half), lambda i: (i, 0, 0, 0)),
            pl.BlockSpec((2, width, half), lambda i: (0, 0, 0)),
        ],
        out_specs=pl.BlockSpec((pairs // GROUP, 1, blocks * 2 * GROUP, wide), lambda i: (0, i, 0, 0)),
        out_shape=jax.ShapeDtypeStruct((pairs // GROUP, 2, blocks * 2 * GROUP, wide), jnp.bfloat16),
        scratch_shapes=[pltpu.VMEM((pl.cdiv(width, LANES), 2, pairs, LANES), jnp.float32)],
        compiler_params=pltpu.CompilerParams(vmem_limit_bytes=24 << 20),
        cost_estimate=pl.CostEstimate(
            flops=2 * 8 * count * half * width,
            bytes_accessed=2 * (waves.size + folds.size),
            transcendentals=0,
        ),
        name="fourier",
    )(waves, folds)


def legendre_kernel(
    half_k, start, extra, place_ref, chunk_ref, within_ref, block_ref, table_ref, keep_ref, send_ref,
    spectra, turned, spare, sems
):
    rows = table_ref.shape[0]
    groups = turned.shape[0]
    width = turned.shape[1] * LANES
    columns = min(width, 2 * half_k + 1 - start)
    _, channels, kept = spectra.shape
    lane = lax.broadcasted_iota(jnp.int32, (channels, LANES), 1)
    def trip(step, carry):
        for group in range(groups):
            first_pair = pl.multiple_of((step * groups + group) * GROUP, GROUP)
            table = table_ref[:, pl.ds(first_pair, GROUP), start : start + columns]
            table = table.reshape(rows * GROUP, columns)
            left = block_ref[step * groups + group].reshape(4 * channels * GROUP, rows * GROUP)
            sums = jnp.dot(left, table, preferred_element_type=jnp.float32)
            sums = sums.reshape(2, 2, channels, GROUP, columns)
            pair = first_pair + lax.broadcasted_iota(jnp.int32, (GROUP, columns), 0)
            column = start + lax.broadcasted_iota(jnp.int32, (GROUP, columns), 1)
            first = column < 2 * half_k - pair
            odd = jnp.where(first, column, column - 2 * half_k + pair) & 1
            even = (odd == 0)[None]
            chosen = jnp.where(
                first[None],
                jnp.where(even, sums[0, 0], sums[0, 1]),
                jnp.where(even, sums[1, 0], sums[1, 1]),
            )
            chosen = chosen.reshape(channels * GROUP, columns)
            for tile in range(width // LANES):
                part = chosen[:, tile * LANES : (tile + 1) * LANES]
                turned[group, tile, :, : part.shape[1]] = part
            for member in range(GROUP):
                place = place_ref[first_pair + member]
                for tile in range(kept // LANES):
                    value = turned[group, tile, pl.ds(member, channels, stride=GROUP), :]
                    spectra[place, :, tile * LANES : (tile + 1) * LANES] = value.astype(spectra.dtype)
                if extra:
                    chunk = chunk_ref[first_pair + member]
                    within = within_ref[first_pair + member]
                    value = turned[group, kept // LANES, pl.ds(member, channels, stride=GROUP), :]
                    value = jnp.broadcast_to(value[:, :1], (channels, LANES))
                    pltpu.store(spare.at[chunk], value, mask=lane == within)
        return carry

    lax.fori_loop(0, half_k // (groups * GROUP), trip, 0)
    if extra:
        stride = spectra.shape[0] // spare.shape[0]
        for chunk in range(spare.shape[0]):
            spectra[(chunk + 1) * stride - 1, :, :LANES] = spare[chunk].astype(spectra.dtype)
    count = spectra.shape[0] // 2
    send = pltpu.make_async_copy(spectra.at[pl.ds(count, count)], send_ref, sems.at[0])
    keep = pltpu.make_async_copy(spectra.at[pl.ds(0, count)], keep_ref, sems.at[1])
    send.start()
    keep.start()
    send.wait()
    keep.wait()


def legendre(places, blocks, table, start, kept, extra, bands, stride):
    rows, half_k, _ = table.shape
    channels = blocks.shape[1] * blocks.shape[2] // (4 * GROUP)
    pairs = 8 * GROUP
    groups = pairs // GROUP
    width = kept + (LANES if extra else 0)
    total = bands * stride
    result = jax.ShapeDtypeStruct((total // 2, channels, kept), jnp.bfloat16)
    return pl.pallas_call(
        functools.partial(legendre_kernel, half_k, start, extra),
        grid_spec=pltpu.PrefetchScalarGridSpec(
            num_scalar_prefetch=3,
            in_specs=[pl.BlockSpec(memory_space=pltpu.VMEM)] * 2,
            out_specs=[pl.BlockSpec(memory_space=pl.ANY)] * 2,
            scratch_shapes=[
                pltpu.VMEM((total, channels, kept), jnp.bfloat16),
                pltpu.VMEM((groups, width // LANES, channels * GROUP, LANES), jnp.float32),
                pltpu.VMEM((bands, channels, LANES), jnp.float32),
                pltpu.SemaphoreType.DMA((2,)),
            ],
        ),
        out_shape=[result, result],
        compiler_params=pltpu.CompilerParams(vmem_limit_bytes=8 << 20),
        cost_estimate=pl.CostEstimate(
            flops=2 * blocks.size * width,
            bytes_accessed=2 * (blocks.size + rows * half_k * width),
            transcendentals=0,
        ),
        name="legendre",
    )(
        *places,
        pltpu.with_memory_space_constraint(blocks, pltpu.VMEM),
        pltpu.with_memory_space_constraint(table, pltpu.VMEM),
    )


def on_device(air, kappa, depth, table, mode_degree):
    levels, _, rows, lon = air.shape
    half_k, columns = table.shape[1:]
    band = lax.axis_index("band")
    bands = lax.axis_size("band")
    bits = bands.bit_length() - 1
    slots = half_k // bands
    steps = 2 * rows * bands

    head, tail = edges(air)
    below = lax.ppermute(head, "band", [(i + 1, i) for i in range(bands - 1)])
    above = lax.ppermute(tail, "band", [(i, i + 1) for i in range(bands - 1)])

    waves = wave_table(lon, columns - 1)
    row = (band * rows + jnp.arange(rows, dtype=jnp.int32)).astype(jnp.float32)[:, None]
    centre = jnp.sin((row + 0.5) * (math.pi / steps))
    up = jnp.sin((row + 1.0) * (math.pi / steps)) / centre
    down = jnp.sin(row * (math.pi / steps)) / centre
    is_last = (band == bands - 1).astype(jnp.int32)[None]
    slot = jnp.arange(half_k, dtype=jnp.int32)
    here = mode_degree[None, :] == slot[:, None]
    relative = (slot // slots) ^ band

    def places_with(order, stride):
        chunk = sum(((relative >> bit) & 1) << (bits - 1 - at) for at, bit in enumerate(order))
        within = slot % slots
        return [
            jnp.sum(jnp.where(here, value[None, :], 0), axis=1, dtype=jnp.int32)
            for value in (chunk * stride + within, chunk, within)
        ]

    smoothed, folds = smooth(air, kappa, above, below, up, down, is_last)
    blocks = fourier_blocks(waves, folds.reshape(2, 2 * levels * rows, lon // 2), rows)
    natural = list(range(bits))
    crossed = natural if bits < 3 else [0, 2, 1, *range(3, bits)]
    top = columns - 1
    streams = []
    for index, start in enumerate(range(0, top, WIDTH)):
        kept = min(WIDTH, top - start)
        extra = start + kept == top
        stride = slots + 1 if extra else slots
        order = crossed if index == 1 else natural
        streams.append(dict(start=start, kept=kept, extra=extra, stride=stride, order=order))

    def outgoing_of(stream):
        count = stream["outgoing"].shape[0] // 2 if "outgoing" in stream else None
        parts = [part[count : 2 * count].astype(jnp.float32) for part in stream["held"]]
        return sum(parts).astype(jnp.bfloat16)

    def send(stream, at, outgoing):
        bit = stream["order"][at]
        stream["outgoing"] = outgoing
        stream["held"].append(
            lax.ppermute(outgoing, "band", [(i, i ^ (1 << bit)) for i in range(bands)])
        )

    previous = None
    for index, stream in enumerate(streams):
        where = places_with(stream["order"], stream["stride"])
        if previous is not None:
            where = lax.optimization_barrier((where, previous))[0]
        keep, outgoing = legendre(
            where, blocks, table, stream["start"], stream["kept"], stream["extra"], bands,
            stream["stride"],
        )
        stream["held"] = [keep]
        send(stream, 0, outgoing)
        previous = [keep]
        if index > 0 and bits > 1:
            earlier = streams[index - 1]
            crossing = outgoing_of(earlier)
            send(earlier, 1, crossing)
            previous.append(crossing)
    if bits > 1:
        send(streams[-1], 1, outgoing_of(streams[-1]))
    for at in range(2, bits):
        for stream in streams:
            send(stream, at, outgoing_of(stream))
    pieces = []
    for stream in streams:
        done = sum(part[: stream["stride"]].astype(jnp.float32) for part in stream["held"])
        pieces.append(done[:slots])
        if stream["extra"]:
            pieces.append(jnp.swapaxes(done[slots, :, :slots], 0, 1)[:, :, None])
    mine = jnp.concatenate(pieces, axis=2)
    mine = mine.reshape(slots, levels, 2, columns)
    weighted = depth[None, :, None, None] * mine
    levs = lax.axis_size("lev")
    total = jnp.sum(weighted, axis=1)
    lower = jnp.zeros_like(total)
    if levs > 1:
        lower = lax.ppermute(total, "lev", [(i + 1, i) for i in range(levs - 1)])
        reach = 1
        while reach < levs - 1:
            lower = lower + lax.ppermute(lower, "lev", [(i + reach, i) for i in range(levs - reach)])
            reach *= 2
    potential = []
    for level in reversed(range(levels)):
        potential.append(lower + 0.5 * weighted[:, level])
        lower = lower + weighted[:, level]
    fields = jnp.stack([mine, jnp.stack(potential[::-1], axis=1)], axis=2)
    return smoothed, jnp.transpose(fields, (1, 2, 3, 0, 4))


def solution(mesh):
    placed = (
        P("lev", None, "band", None),
        P(None, "band", None),
        P("lev"),
        P("band", None, None),
        P(),
    )
    return jax.shard_map(
        on_device,
        mesh=mesh,
        in_specs=placed,
        out_specs=(P("lev", None, "band", None), P("lev", None, None, "band", None)),
        check_vma=False,
    )
```
